128 devices in a mesh: dp: 4 (over x), tensor: 4 (over z), opt: 8 (over y, core).
Axes of the slice: x: 4, y: 4, z: 4, core: 2. Of those that a mesh axis runs over, the one named last changes fastest.
Arguments:
- inputs: bfloat16 [4096, 4096], P(('dp', 'tensor', 'opt')), may hold values from -6 to 6
- cotangent: bfloat16 [4096, 4096], P(('dp', 'tensor', 'opt')), may hold values from -6 to 6
- w_gate: bfloat16 [14336, 4096], P(('tensor', 'opt')), may hold values from -0.09375 to 0.09375
- w_up: bfloat16 [14336, 4096], P(('tensor', 'opt')), may hold values from -0.09375 to 0.09375
- w_down: bfloat16 [14336, 4096], P(('tensor', 'opt')), may hold values from -0.046875 to 0.046875
- chosen: int32 [32, 128], P(('tensor', 'opt')), may hold values from 0 to 447, as said below
- live_rows: int32 [32], P(('tensor', 'opt')), may hold values from 32 to 128, as said below
- master: float32 [32, 128, 3, 4096], P(('tensor', 'opt'), None, None, 'dp'), may hold values from -0.3 to 0.3
- moment_one: float32 [32, 128, 3, 4096], P(('tensor', 'opt'), None, None, 'dp'), may hold values from -2 to 2
- moment_two: float32 [32, 128, 3, 4096], P(('tensor', 'opt'), None, None, 'dp'), may hold values from 0.05 to 0.5
Outputs:
- input_grad: bfloat16 [4096, 4096], P(('dp', 'tensor', 'opt'))
- new_master: float32 [32, 128, 3, 4096], P(('tensor', 'opt'), None, None, 'dp')
- new_moment_one: float32 [32, 128, 3, 4096], P(('tensor', 'opt'), None, None, 'dp')
- new_moment_two: float32 [32, 128, 3, 4096], P(('tensor', 'opt'), None, None, 'dp')
The draws below stay inside these ranges and needn't reach their ends.
Inputs may be any that keep to these rules, and one draw needn't show every extreme that they name: `chosen`: within one shard the 128 entries are distinct hidden units of that shard. `live_rows`: some shard uses all 128 slots and some shard only 32.
All inputs are finite; a program needn't handle non-finite values.
Results may differ from the reference program's by a relative error of at most 0.023.
Values may be sent and summed in bfloat16 or wider, within the bound.
A program may use at most 192 MiB of HBM per device.

```python
import math
import jax
import jax.numpy as jnp
from jax import lax

D = 4096
FF = 14336
CAP = 128
TOKENS = 4096
SHARDS = 32
FF_DEV = 448


def draw_chosen(key, part):
    keys = jax.random.split(key, SHARDS)
    perms = jax.vmap(lambda single: jax.random.permutation(single, FF_DEV))(keys)
    return perms[:, :CAP].astype(jnp.int32)


def draw_live_rows(key, part):
    counts = jax.random.randint(jax.random.fold_in(key, 11), (SHARDS,), CAP // 4, CAP + 1)
    order = jax.random.permutation(jax.random.fold_in(key, 12), SHARDS)
    counts = counts.at[order[0]].set(CAP)
    counts = counts.at[order[1]].set(CAP // 4)
    return counts.astype(jnp.int32)


def shard_levels(key, shape, cuts, least, largest):
    factor_of = 1.0
    for position, blocks in cuts:
        steps = jax.random.uniform(jax.random.fold_in(jax.random.fold_in(key, 6), position), (blocks,), jnp.float32, least / len(cuts), largest / len(cuts))
        factor_of = factor_of * jnp.repeat(jnp.exp(steps), shape[position] // blocks).reshape((-1,) + (1,) * (len(shape) - 1 - position))
    return factor_of


def normal_values(key, dims, width, most, pieces=(), kind=jnp.bfloat16):
    values = jax.random.normal(key, dims, jnp.float32) * width
    if len(pieces) > 0:
        values = shard_levels(key, dims, pieces, -0.22, 0.18) * values
    return jnp.clip(values, min=-most, max=most).astype(kind)


def setup_inputs(seed: int = 0) -> dict:
    seeds = jax.random.split(jax.random.key(seed), 11)
    return {
        "inputs": normal_values(seeds[0], (TOKENS, D), 1.0, 6.0, ((0, 128),)),
        "cotangent": normal_values(seeds[1], (TOKENS, D), 1.0, 6.0, ((0, 128),)),
        "w_gate": normal_values(seeds[2], (FF, D), D ** -0.5, 0.09375, ((0, 32),)),
        "w_up": normal_values(seeds[3], (FF, D), D ** -0.5, 0.09375, ((0, 32),)),
        "w_down": normal_values(seeds[4], (FF, D), FF ** -0.5, 0.046875, ((0, 32),)),
        "chosen": draw_chosen(jax.random.fold_in(seeds[10], 71), 0),
        "live_rows": draw_live_rows(jax.random.fold_in(seeds[10], 71), 0),
        "master": normal_values(seeds[7], (SHARDS, CAP, 3, D), 0.05, 0.3, ((0, 32), (3, 4)), jnp.float32),
        "moment_one": normal_values(seeds[8], (SHARDS, CAP, 3, D), 0.3, 2.0, ((0, 32), (3, 4)), jnp.float32),
        "moment_two": jnp.clip(jnp.exp(math.log(0.5) - 2.3025851 * jax.random.uniform(seeds[9], (SHARDS, CAP, 3, D), jnp.float32) ** shard_levels(seeds[9], (SHARDS, CAP, 3, D), ((0, 32), (3, 4)), -0.2, 0.2)), 0.05, 0.5),
    }


def math_sqrt(value):
    return float(value) ** 0.5

def reference(inputs, cotangent, w_gate, w_up, w_down, chosen, live_rows, master, moment_one, moment_two):
    gate_val = jnp.dot(inputs, w_gate.T, preferred_element_type=jnp.float32)
    up_val = jnp.dot(inputs, w_up.T, preferred_element_type=jnp.float32)
    sig_gate = jax.nn.sigmoid(gate_val)
    activ = gate_val * sig_gate
    hidden = (activ * up_val).astype(jnp.bfloat16)
    hidden_grad = jnp.dot(cotangent, w_down.T, preferred_element_type=jnp.float32)
    gate_grad = (hidden_grad * up_val * sig_gate * (1.0 + gate_val * (1.0 - sig_gate))).astype(jnp.bfloat16)
    up_grad = (hidden_grad * activ).astype(jnp.bfloat16)

    def add_shard(index, total):
        start = (index * FF_DEV).astype(jnp.int32)
        gate_part = lax.dynamic_slice_in_dim(gate_grad, start, FF_DEV, 1)
        up_part = lax.dynamic_slice_in_dim(up_grad, start, FF_DEV, 1)
        gate_rows = lax.dynamic_slice_in_dim(w_gate, start, FF_DEV, 0)
        up_rows = lax.dynamic_slice_in_dim(w_up, start, FF_DEV, 0)
        term = (jnp.dot(gate_part, gate_rows, preferred_element_type=jnp.float32) + jnp.dot(up_part, up_rows, preferred_element_type=jnp.float32)).astype(jnp.bfloat16)
        return total + term.astype(jnp.float32)
    summed = lax.fori_loop(jnp.int32(0), jnp.int32(SHARDS), add_shard, jnp.zeros((TOKENS, D), jnp.float32))
    input_grad = summed.astype(jnp.bfloat16)
    shard_base = (jnp.arange(SHARDS, dtype=jnp.int32) * FF_DEV)[:, None]
    unit_index = (shard_base + chosen.astype(jnp.int32)).reshape(-1)
    sel_gate = jnp.take(gate_grad, unit_index, axis=1)
    sel_up = jnp.take(up_grad, unit_index, axis=1)
    sel_hidden = jnp.take(hidden, unit_index, axis=1)
    grad_gate = jnp.dot(sel_gate.T, inputs, preferred_element_type=jnp.float32)
    grad_up = jnp.dot(sel_up.T, inputs, preferred_element_type=jnp.float32)
    grad_down = jnp.dot(sel_hidden.T, cotangent, preferred_element_type=jnp.float32)
    row_grad = jnp.stack([grad_gate, grad_up, grad_down], axis=1).reshape(SHARDS, CAP, 3, D)
    row_grad = row_grad * (1.0 / math_sqrt(TOKENS))
    first = 0.9 * moment_one + 0.1 * row_grad
    second = 0.95 * moment_two + 0.05 * row_grad * row_grad
    corr_one = 1.0 - 0.9 ** 10
    corr_two = 1.0 - 0.95 ** 10
    update = 0.01 * (first / corr_one) / (jnp.sqrt(second / corr_two) + 1e-08)
    in_use = (jnp.arange(CAP, dtype=jnp.int32)[None, :] < live_rows[:, None])[:, :, None, None]
    new_master = jnp.where(in_use, master - update, master)
    new_moment_one = jnp.where(in_use, first, moment_one)
    new_moment_two = jnp.where(in_use, second, moment_two)
    return (input_grad, new_master, new_moment_one, new_moment_two)
```

```python
import functools

import jax
import jax.numpy as jnp
from jax import lax
from jax.experimental import pallas as pl
from jax.experimental.pallas import tpu as pltpu
from jax.sharding import PartitionSpec as P

MESH = pl.DeviceIdType.MESH
F32, BF16 = jnp.float32, jnp.bfloat16
NT = (((1,), (1,)), ((), ()))
CHUNK = 1024
TILE = 256


class Messages:
    def __init__(self, send, recv):
        self.send, self.recv, self.all = send, recv, []

    def go(self, src, dst, device):
        i = len(self.all)
        copy = pltpu.make_async_remote_copy(
            src_ref=src,
            dst_ref=dst,
            send_sem=self.send.at[i],
            recv_sem=self.recv.at[i],
            device_id=device,
            device_id_type=MESH,
        )
        copy.start()
        self.all.append(copy)
        return copy


def kernel(
    inputs, cot, w_gate, w_up, w_down, chosen,
    grad_out, rows_out,
    xc, wg, wu, wd, wgs, wus, own_g, own_u, put_g, put_u, got_g, got_u,
    racc, xs1, xs2p, xs2m, xr1p, xr1m, xr2p, xr2m,
    psum, r11p, r11m, r12p, r12m, r21p, r21m, r22p, r22m,
    lsem, send, recv,
):
    dp, tz, op = lax.axis_index("dp"), lax.axis_index("tensor"), lax.axis_index("opt")
    y, core = op // 2, op % 2
    hidden_units = wg.shape[0]
    slots = racc.shape[1]
    width = wg.shape[1]
    quarter = width // 4

    def up(i):
        return (i + 1) % 4

    def down(i):
        return (i + 3) % 4

    xp, xm = (up(dp), tz, op), (down(dp), tz, op)
    yp, ym = (dp, tz, up(y) * 2 + core), (dp, tz, down(y) * 2 + core)
    zp, zm = (dp, up(tz), op), (dp, down(tz), op)
    sib = (dp, tz, y * 2 + 1 - core)
    first = ((yp, ym), (zp, zm))
    second = ((zp, zm), (yp, ym))

    local = []

    def bring(src, dst):
        copy = pltpu.make_async_copy(src, dst, lsem.at[len(local)])
        copy.start()
        local.append(copy)
        return copy

    mine = []
    for half in range(2):
        for kind, ref in enumerate((inputs, cot)):
            mine.append(bring(ref.at[pl.ds(half * 16, 16)], xc.at[kind, 0, half, 0, 0]))
    weights = [bring(w_gate, wg), bring(w_up, wu), bring(w_down, wd)]

    barrier = pltpu.get_barrier_semaphore()
    for peer in (xp, xm, yp, ym, zp, zm, sib):
        pl.semaphore_signal(barrier, inc=1, device_id=peer, device_id_type=MESH)
    pl.semaphore_wait(barrier, 7)
    for copy in mine:
        copy.wait()

    net = Messages(send, recv)

    def ahead(half, k2, k1):
        return xc.at[:, k2, half, k1, 0]

    one_p, one_m, two_in, two_cot = {}, {}, {}, {}
    far_p, far_m, far_in, far_cot = {}, {}, {}, {}
    shared = {}

    def share(half, k2, k1):
        shared[half, k2, k1] = net.go(ahead(half, k2, k1), xc.at[:, k2, half, k1, 1], sib)

    def across(half, k1):
        here = ahead(half, 0, k1)
        far_p[half, k1] = net.go(here, ahead(half, 3, k1), second[half][0])
        far_m[half, k1] = net.go(here, ahead(half, 1, k1), second[half][1])

    for half in range(2):
        here = ahead(half, 0, 0)
        one_p[half] = net.go(here, ahead(half, 0, 3), first[half][0])
        one_m[half] = net.go(here, ahead(half, 0, 1), first[half][1])
    for half in range(2):
        across(half, 0)
        share(half, 0, 0)
    for half in range(2):
        one_p[half].wait_recv()
        two_in[half] = net.go(xc.at[0, 0, half, 3, 0], xc.at[0, 0, half, 2, 0], first[half][0])
        one_m[half].wait_recv()
        two_cot[half] = net.go(xc.at[1, 0, half, 1, 0], xc.at[1, 0, half, 2, 0], first[half][1])
    for half in range(2):
        for k1 in (3, 1):
            across(half, k1)
            share(half, 0, k1)
    for half in range(2):
        two_in[half].wait_recv()
        two_cot[half].wait_recv()
        across(half, 2)
        share(half, 0, 2)
    sib_gate = net.go(w_gate, wgs, sib)
    sib_up = net.go(w_up, wus, sib)

    unit = lax.broadcasted_iota(jnp.int32, (slots, hidden_units), 1)
    pick = (unit == chosen[...]).astype(F32).astype(BF16)
    passed = {}

    def block(k2):
        for half in range(2):
            for k1 in range(4):
                shared[half, k2, k1].wait_recv()
        tokens = 2 * 4 * 2 * 16
        x = xc[0, k2].reshape(tokens, width)
        c = xc[1, k2].reshape(tokens, width)
        gate = lax.dot_general(x, wg[...], NT, preferred_element_type=F32)
        upv = lax.dot_general(x, wu[...], NT, preferred_element_type=F32)
        back = lax.dot_general(c, wd[...], NT, preferred_element_type=F32)
        sig = jax.nn.sigmoid(gate)
        activ = gate * sig
        hid = (activ * upv).astype(BF16)
        gg = (back * upv * sig * (1.0 + gate * (1.0 - sig))).astype(BF16)
        ug = (back * activ).astype(BF16)
        for value, own, put in ((gg, own_g, put_g), (ug, own_u, put_u)):
            split = value.reshape(8, 2, 16, hidden_units)
            own[k2] = split[:, 0].reshape(128, hidden_units)
            put[k2] = split[:, 1].reshape(128, hidden_units)
        passed[k2] = (net.go(put_g.at[k2], got_g.at[k2], sib), net.go(put_u.at[k2], got_u.at[k2], sib))
        for kind, (value, rows) in enumerate(((gg, x), (ug, x), (hid, c))):
            sel = lax.dot_general(pick, value, NT, preferred_element_type=F32).astype(BF16)
            part = jnp.dot(sel, rows, preferred_element_type=F32)
            if k2 == 0:
                racc[kind] = part
            else:
                racc[kind] += part

    for copy in weights:
        copy.wait()
    block(0)

    for k1 in (0, 3, 1, 2):
        for half in range(2):
            far_p[half, k1].wait_recv()
            far_in[half, k1] = net.go(xc.at[0, 3, half, k1, 0], xc.at[0, 2, half, k1, 0], second[half][0])
            share(half, 3, k1)
            far_m[half, k1].wait_recv()
            far_cot[half, k1] = net.go(xc.at[1, 1, half, k1, 0], xc.at[1, 2, half, k1, 0], second[half][1])
            share(half, 1, k1)

    def last(k1):
        for half in range(2):
            far_in[half, k1].wait_recv()
            far_cot[half, k1].wait_recv()
            share(half, 2, k1)

    block(3)
    last(0)
    last(3)
    block(1)
    last(1)
    last(2)
    block(2)

    def part_of(k):
        return pl.ds(pl.multiple_of(((dp + k) % 4) * quarter, quarter), quarter)

    lo, hi = slice(0, slots // 2), slice(slots // 2, slots)
    xs1[...] = racc[:, :, part_of(2)].astype(BF16)
    x1p = net.go(xs1.at[:, lo], xr1p, xp)
    x1m = net.go(xs1.at[:, hi], xr1m, xm)

    sib_gate.wait_recv()
    sib_up.wait_recv()
    for pair in passed.values():
        for copy in pair:
            copy.wait_recv()

    def chunk_sums(j):
        def tile(i, carry):
            at = pl.ds(pl.multiple_of(j * CHUNK + i * TILE, TILE), TILE)
            total = jnp.zeros((512, TILE), F32)
            for grads, weight in ((own_g, wg), (own_u, wu), (got_g, wgs), (got_u, wus)):
                total += jnp.dot(
                    grads[...].reshape(512, hidden_units), weight[:, at], preferred_element_type=F32
                )
            psum[:, :, :, :, at] = total.astype(BF16).reshape(4, 2, 4, 16, TILE)
            return carry

        lax.fori_loop(0, CHUNK // TILE, tile, 0)

    flows = [{} for _ in range(width // CHUNK)]

    def add(*parts):
        total = parts[0].astype(F32)
        for part in parts[1:]:
            total += part.astype(F32)
        return total.astype(BF16)

    def spans(j):
        mid = CHUNK // 2
        whole = pl.ds(j * CHUNK, CHUNK)
        return whole, pl.ds(j * CHUNK, mid), pl.ds(j * CHUNK + mid, mid), pl.ds(j * mid, mid)

    def stage0(j):
        chunk_sums(j)
        whole, a, b, s = spans(j)
        for half in range(2):
            flows[j][0, half] = (
                net.go(psum.at[2, half, :, :, a], r11p.at[half, :, :, s], second[half][0]),
                net.go(psum.at[2, half, :, :, b], r11m.at[half, :, :, s], second[half][1]),
            )

    def stage1(j):
        whole, a, b, s = spans(j)
        for half in range(2):
            p, m = flows[j][0, half]
            p.wait_recv()
            psum[1, half, :, :, a] = add(psum[1, half, :, :, a], r11p[half, :, :, s])
            fp = net.go(psum.at[1, half, :, :, whole], r12p.at[half, :, :, whole], second[half][0])
            m.wait_recv()
            psum[3, half, :, :, b] = add(psum[3, half, :, :, b], r11m[half, :, :, s])
            fm = net.go(psum.at[3, half, :, :, whole], r12m.at[half, :, :, whole], second[half][1])
            flows[j][1, half] = (fp, fm)

    def stage2(j):
        whole, a, b, s = spans(j)
        for half in range(2):
            for copy in flows[j][1, half]:
                copy.wait_recv()
            psum[0, half, :, :, whole] = add(
                psum[0, half, :, :, whole], r12p[half, :, :, whole], r12m[half, :, :, whole]
            )
            flows[j][2, half] = (
                net.go(psum.at[0, half, 2, :, a], r21p.at[half, :, s], first[half][0]),
                net.go(psum.at[0, half, 2, :, b], r21m.at[half, :, s], first[half][1]),
            )

    def stage3(j):
        whole, a, b, s = spans(j)
        for half in range(2):
            p, m = flows[j][2, half]
            p.wait_recv()
            psum[0, half, 1, :, a] = add(psum[0, half, 1, :, a], r21p[half, :, s])
            fp = net.go(psum.at[0, half, 1, :, whole], r22p.at[half, :, whole], first[half][0])
            m.wait_recv()
            psum[0, half, 3, :, b] = add(psum[0, half, 3, :, b], r21m[half, :, s])
            fm = net.go(psum.at[0, half, 3, :, whole], r22m.at[half, :, whole], first[half][1])
            flows[j][3, half] = (fp, fm)

    def stage4(j):
        whole, a, b, s = spans(j)
        for half in range(2):
            for copy in flows[j][3, half]:
                copy.wait_recv()
            grad_out[half * 16 : half * 16 + 16, whole] = add(
                psum[0, half, 0, :, whole], r22p[half, :, whole], r22m[half, :, whole]
            )

    x2 = []

    def x_middle():
        x1p.wait_recv()
        value = racc[:, :, part_of(1)]
        xs2p[:, hi] = value[:, hi].astype(BF16)
        xs2p[:, lo] = (value[:, lo] + xr1p[...].astype(F32)).astype(BF16)
        x2.append(net.go(xs2p, xr2p, xp))
        x1m.wait_recv()
        value = racc[:, :, part_of(3)]
        xs2m[:, lo] = value[:, lo].astype(BF16)
        xs2m[:, hi] = (value[:, hi] + xr1m[...].astype(F32)).astype(BF16)
        x2.append(net.go(xs2m, xr2m, xm))

    stages = (stage0, stage1, stage2, stage3, stage4)
    n = len(flows)
    for step in range(n + len(stages) - 1):
        for s, stage in enumerate(stages):
            if 0 <= step - s < n:
                stage(step - s)
        if step == 2:
            x_middle()
    for copy in x2:
        copy.wait_recv()
    rows_out[...] = (
        racc[:, :, part_of(0)] + xr2p[...].astype(F32) + xr2m[...].astype(F32)
    ).astype(rows_out.dtype)
    for copy in net.all:
        copy.wait_send()


def exchange(inputs, cotangent, w_gate, w_up, w_down, chosen, slots):
    units, width = w_gate.shape
    grads = (4, 128, units)
    quarter = (3, slots, width // 4)
    half_quarter = (3, slots // 2, width // 4)
    any_space = pl.BlockSpec(memory_space=pl.ANY)
    vmem = pl.BlockSpec(memory_space=pltpu.VMEM)
    messages = 72 + 2 + 8 + 4 + 16 * (width // CHUNK)
    return pl.pallas_call(
        kernel,
        out_shape=(
            jax.ShapeDtypeStruct((32, width), BF16),
            jax.ShapeDtypeStruct(quarter, BF16),
        ),
        in_specs=[any_space] * 5 + [vmem],
        out_specs=(vmem, vmem),
        scratch_shapes=[
            pltpu.VMEM((2, 4, 2, 4, 2, 16, width), BF16),
            pltpu.VMEM((units, width), BF16),
            pltpu.VMEM((units, width), BF16),
            pltpu.VMEM((units, width), BF16),
            pltpu.VMEM((units, width), BF16),
            pltpu.VMEM((units, width), BF16),
            pltpu.VMEM(grads, BF16),
            pltpu.VMEM(grads, BF16),
            pltpu.VMEM(grads, BF16),
            pltpu.VMEM(grads, BF16),
            pltpu.VMEM(grads, BF16),
            pltpu.VMEM(grads, BF16),
            pltpu.VMEM((3, slots, width), F32),
            pltpu.VMEM(quarter, BF16),
            pltpu.VMEM(quarter, BF16),
            pltpu.VMEM(quarter, BF16),
            pltpu.VMEM(half_quarter, BF16),
            pltpu.VMEM(half_quarter, BF16),
            pltpu.VMEM(quarter, BF16),
            pltpu.VMEM(quarter, BF16),
            pltpu.VMEM((4, 2, 4, 16, width), BF16),
            pltpu.VMEM((2, 4, 16, width // 2), BF16),
            pltpu.VMEM((2, 4, 16, width // 2), BF16),
            pltpu.VMEM((2, 4, 16, width), BF16),
            pltpu.VMEM((2, 4, 16, width), BF16),
            pltpu.VMEM((2, 16, width // 2), BF16),
            pltpu.VMEM((2, 16, width // 2), BF16),
            pltpu.VMEM((2, 16, width), BF16),
            pltpu.VMEM((2, 16, width), BF16),
            pltpu.SemaphoreType.DMA((7,)),
            pltpu.SemaphoreType.DMA((messages,)),
            pltpu.SemaphoreType.DMA((messages,)),
        ],
        compiler_params=pltpu.CompilerParams(
            collective_id=0, has_side_effects=True, vmem_limit_bytes=64 * 1024 * 1024 - 64 * 1024
        ),
    )(inputs, cotangent, w_gate, w_up, w_down, chosen)


def local(
    inputs, cotangent, w_gate, w_up, w_down, chosen, live_rows, master, moment_one, moment_two
):
    slots = chosen.shape[1]
    input_grad, row_grad = exchange(
        inputs, cotangent, w_gate, w_up, w_down, chosen.reshape(slots, 1), slots
    )
    total_tokens = inputs.shape[0] * 128
    row_grad = jnp.transpose(row_grad, (1, 0, 2)).astype(F32)
    row_grad = (row_grad * (1.0 / float(total_tokens) ** 0.5))[None]
    first = 0.9 * moment_one + 0.1 * row_grad
    second = 0.95 * moment_two + 0.05 * row_grad * row_grad
    corr_one = 1.0 - 0.9**10
    corr_two = 1.0 - 0.95**10
    update = 0.01 * (first / corr_one) / (jnp.sqrt(second / corr_two) + 1e-08)
    in_use = (jnp.arange(slots, dtype=jnp.int32)[None, :] < live_rows[:, None])[:, :, None, None]
    return (
        input_grad,
        jnp.where(in_use, master - update, master),
        jnp.where(in_use, first, moment_one),
        jnp.where(in_use, second, moment_two),
    )


def solution(mesh):
    token = P(("dp", "tensor", "opt"), None)
    hidden = P(("tensor", "opt"), None)
    state = P(("tensor", "opt"), None, None, "dp")
    return jax.shard_map(
        local,
        mesh=mesh,
        in_specs=(
            token, token, hidden, hidden, hidden, hidden, P(("tensor", "opt")), state, state, state,
        ),
        out_specs=(token, state, state, state),
        check_vma=False,
    )
```

```python
import jax
import jax.numpy as jnp
from jax import lax
from jax.experimental import pallas as pl
from jax.experimental.pallas import tpu as pltpu
from jax.sharding import PartitionSpec as P

MESH = pl.DeviceIdType.MESH
F32, BF16 = jnp.float32, jnp.bfloat16
NT = (((1,), (1,)), ((), ()))
CHUNK = 1024
TILE = 512
ORDER = (0, 1, 3, 2)
SENDS, RECEIVES = 16, 112
TOKENS = 4096
ADAM_COLUMNS = 1024


def kernel(
    inputs, cot, w_gate, w_up, w_down, chosen,
    grad_out, rows_out,
    xc, wg, wu, wd, wgs, wus, own_g, own_u, put_g, put_u, got_g, got_u,
    racc, xs1, xs2p, xs2m, xr1p, xr1m, xr2p, xr2m,
    r1p, r1m, r1f, r2p, r2m, r2f,
    rows_here, lsem, send, recv,
):
    dp, tz, op = lax.axis_index("dp"), lax.axis_index("tensor"), lax.axis_index("opt")
    y, core = op // 2, op % 2
    units, width = wg.shape
    slots = racc.shape[1]
    quarter = width // 4

    def on(i, k):
        return (i + k) % 4

    xp, xm = (on(dp, 1), tz, op), (on(dp, 3), tz, op)
    yp, ym, yf = ((dp, tz, on(y, k) * 2 + core) for k in (1, 3, 2))
    zp, zm, zf = ((dp, on(tz, k), op) for k in (1, 3, 2))
    sib = (dp, tz, y * 2 + 1 - core)
    first = ((yp, ym, yf), (zp, zm, zf))
    second = ((zp, zm, zf), (yp, ym, yf))

    psum = xc.at[0, :, :, :, 1]
    brought = []

    def bring(src, dst):
        copy = pltpu.make_async_copy(src, dst, lsem.at[len(brought)])
        copy.start()
        brought.append(copy)
        return copy

    mine = []
    for half in range(2):
        for kind, ref in enumerate((inputs, cot)):
            mine.append(bring(ref.at[pl.ds(half * 16, 16)], xc.at[kind, 0, half, 0, 0]))

    barrier = pltpu.get_barrier_semaphore()
    peers = (xp, xm, yp, ym, yf, zp, zm, zf, sib)
    for peer in peers:
        pl.semaphore_signal(barrier, inc=1, device_id=peer, device_id_type=MESH)
    pl.semaphore_wait(barrier, len(peers))

    groups, arrivals = [], []

    def group(total):
        groups.append((send.at[len(groups)], total))
        return groups[-1][0]

    def arrival():
        arrivals.append(None)
        return recv.at[len(arrivals) - 1]

    def copy_of(src, dst, s, r, device):
        return pltpu.make_async_remote_copy(
            src_ref=src, dst_ref=dst, send_sem=s, recv_sem=r, device_id=device, device_id_type=MESH
        )

    def go(src, dst, s, device, r=None):
        copy = copy_of(src, dst, s, arrival() if r is None else r, device)
        copy.start()
        return copy

    def all_of(dst, r):
        return copy_of(dst, dst, groups[0][0], r, sib)

    s_one = group(xc.at[0, 0, 0])
    s_two = group(xc.at[0, 0, 0, pl.ds(0, 2)])
    s_far = group(xc.at[:, 0])
    s_farther = group(xc.at[0, 0])
    s_share = group(xc.at[:, :, :, :, 0])
    s_wg, s_wu = group(wgs), group(wus)
    s_g, s_u = group(put_g), group(put_u)
    s_x1, s_x2p, s_x2m = group(xs1), group(xs2p), group(xs2m)
    s_near, s_last, s_row = group(psum.at[pl.ds(1, 2)]), group(psum.at[3]), group(psum.at[0, :, pl.ds(1, 3)])

    pieces = {
        "near": (slice(0, 1), slice(0, 4)),
        "mid0": (slice(1, 3), slice(0, 2)),
        "mid1": (slice(1, 3), slice(2, 4)),
        "last": (slice(3, 4), slice(0, 4)),
    }
    shared = {}
    for name in pieces:
        shared[name] = arrival()

    def ds(s):
        return pl.ds(s.start, s.stop - s.start)

    def piece_of(k2, k1):
        for name, (a, b) in pieces.items():
            if a.start <= k2 < a.stop and b.start <= k1 < b.stop:
                return name

    def slot(half, k2, k1):
        return xc.at[:, k2, half, k1, 0]

    def share(half, k2, k1):
        go(slot(half, k2, k1), xc.at[:, k2, half, k1, 1], s_share, sib, shared[piece_of(k2, k1)])

    one_p, one_m, two_in, two_cot = {}, {}, {}, {}
    far_p, far_m, far_in, far_cot = {}, {}, {}, {}

    def across(half, k1):
        here = slot(half, 0, k1)
        far_p[half, k1] = go(here, slot(half, 2, k1), s_far, second[half][0])
        far_m[half, k1] = go(here, slot(half, 1, k1), s_far, second[half][1])

    for half in range(2):
        for kind, ref in enumerate((inputs, cot)):
            here = ref.at[pl.ds(half * 16, 16)]
            one_p[half, kind] = go(here, xc.at[kind, 0, half, 2, 0], s_one, first[half][0])
            one_m[half, 1 - kind] = go(here, xc.at[kind, 0, half, 1, 0], s_one, first[half][1])
    for copy in mine:
        copy.wait()
    for half in range(2):
        across(half, 0)
    for half in range(2):
        share(half, 0, 0)
    sib_gate = go(w_gate, wgs, s_wg, sib)
    sib_up = go(w_up, wus, s_wu, sib)
    weights = [bring(w_gate, wg), bring(w_up, wu), bring(w_down, wd)]
    unit = lax.broadcasted_iota(jnp.int32, (512, slots), 0)
    pick = jnp.transpose((unit == chosen[...]).astype(F32))[:, :units].astype(BF16)
    for half in range(2):
        one_p[half, 0].wait_recv()
        two_in[half] = go(xc.at[0, 0, half, 2, 0], xc.at[0, 0, half, 3, 0], s_two, first[half][0])
        one_m[half, 0].wait_recv()
        two_cot[half] = go(xc.at[1, 0, half, 1, 0], xc.at[1, 0, half, 3, 0], s_two, first[half][1])
    for k1, side in ((1, one_m), (2, one_p)):
        for half in range(2):
            side[half, 1].wait_recv()
            across(half, k1)
            share(half, 0, k1)
    for half in range(2):
        two_in[half].wait_recv()
        two_cot[half].wait_recv()
        across(half, 3)
        share(half, 0, 3)

    sums = {"near": (arrival(), arrival()), "mid": (arrival(), arrival()), "last": (arrival(), arrival())}

    def part_of(k):
        return pl.ds(pl.multiple_of(on(dp, k) * quarter, quarter), quarter)

    lo, hi = slice(0, slots // 2), slice(slots // 2, slots)
    x1 = []

    def forward(name):
        a, b = pieces[name]
        na, nb = a.stop - a.start, b.stop - b.start
        tokens = na * 2 * nb * 2 * 16
        all_of(xc.at[:, ds(a), :, ds(b), 1], shared[name]).wait_recv()
        x = xc[0, a, :, b].reshape(tokens, width)
        c = xc[1, a, :, b].reshape(tokens, width)
        ends = sums[name.rstrip("01")]
        picked = [0.0, 0.0, 0.0]
        for u in (slice(0, 256), slice(256, units)):
            gate = lax.dot_general(x, wg[u], NT, preferred_element_type=F32)
            upv = lax.dot_general(x, wu[u], NT, preferred_element_type=F32)
            back = lax.dot_general(c, wd[u], NT, preferred_element_type=F32)
            sig = jax.nn.sigmoid(gate)
            activ = gate * sig
            hid = (activ * upv).astype(BF16)
            gg = (back * upv * sig * (1.0 + gate * (1.0 - sig))).astype(BF16)
            ug = (back * activ).astype(BF16)
            for value, own, put in ((gg, own_g, put_g), (ug, own_u, put_u)):
                split = value.reshape(na * 2 * nb, 2, 16, u.stop - u.start)
                own[a, :, b, :, u] = split[:, 0].reshape(na, 2, nb, 16, u.stop - u.start)
                put[a, :, b, :, u] = split[:, 1].reshape(na, 2, nb, 16, u.stop - u.start)
            for i, value in enumerate((gg, ug, hid)):
                picked[i] += lax.dot_general(pick[:, u], value, NT, preferred_element_type=F32)
        for put, got, s, r in ((put_g, got_g, s_g, ends[0]), (put_u, got_u, s_u, ends[1])):
            for k2 in range(a.start, a.stop):
                go(put.at[k2, :, ds(b)], got.at[k2, :, ds(b)], s, sib, r)
        picked = [value.astype(BF16) for value in picked]
        both = jnp.concatenate(picked[:2], axis=0)
        if name != "last":
            part = jnp.dot(both, x, preferred_element_type=F32).reshape(2, slots, width)
            down = jnp.dot(picked[2], c, preferred_element_type=F32)
            if name == "near":
                racc[0:2] = part
                racc[2] = down
            else:
                racc[0:2] += part
                racc[2] += down
            return
        for k in (2, 1, 3, 0):
            at = part_of(k)
            for kinds, rows, values in ((2, 0, both), (1, 1, picked[2])):
                rows = xc[rows, a, :, b, :, :, at].reshape(tokens, quarter)
                part = jnp.dot(values, rows, preferred_element_type=F32).reshape(kinds, slots, quarter)
                for i in range(kinds):
                    kind = i if kinds == 2 else 2
                    total = racc[kind, :, at] + part[i]
                    if k != 2:
                        racc[kind, :, at] = total
                        continue
                    xs1[kind] = total.astype(BF16)
                    x1.append(
                        (
                            go(xs1.at[kind, ds(lo)], xr1p.at[kind], s_x1, xp),
                            go(xs1.at[kind, ds(hi)], xr1m.at[kind], s_x1, xm),
                        )
                    )

    def sum_chip(a, start, stop):
        rows = (a.stop - a.start) * 128

        def tile(i, carry):
            at = pl.ds(pl.multiple_of(start + i * TILE, TILE), TILE)
            total = jnp.zeros((rows, TILE), F32)
            for grads, weight in ((own_g, wg), (own_u, wu), (got_g, wgs), (got_u, wus)):
                total += jnp.dot(grads[a].reshape(rows, units), weight[:, at], preferred_element_type=F32)
            psum[a, :, :, :, at] = total.astype(BF16).reshape(a.stop - a.start, 2, 4, 16, TILE)
            return carry

        lax.fori_loop(0, (stop - start) // TILE, tile, 0)

    def passed(name, a):
        for got, r in zip((got_g, got_u), sums[name]):
            all_of(got.at[ds(a)], r).wait_recv()

    def onward(k1):
        for half in range(2):
            far_p[half, k1].wait_recv()
            far_in[half, k1] = go(xc.at[0, 2, half, k1, 0], xc.at[0, 3, half, k1, 0], s_farther, second[half][0])
            share(half, 2, k1)
            far_m[half, k1].wait_recv()
            far_cot[half, k1] = go(xc.at[1, 1, half, k1, 0], xc.at[1, 3, half, k1, 0], s_farther, second[half][1])
            share(half, 1, k1)

    def landed(k1):
        for half in range(2):
            far_in[half, k1].wait_recv()
            far_cot[half, k1].wait_recv()
            share(half, 3, k1)

    near, mid, last = slice(0, 1), slice(1, 3), slice(3, 4)
    for copy in weights:
        copy.wait()
    forward("near")
    onward(0)
    passed("near", near)
    sib_gate.wait_recv()
    sib_up.wait_recv()
    sum_chip(near, 0, width)
    onward(1)
    forward("mid0")
    onward(2)
    onward(3)
    forward("mid1")
    landed(0)
    landed(1)
    passed("mid", mid)
    landed(2)
    sum_chip(mid, 0, width // 2)
    landed(3)
    sum_chip(mid, width // 2, width)
    flow = {}
    for half in range(2):
        flow["p", half] = go(psum.at[1, half], r1p.at[half], s_near, second[half][0])
        flow["m", half] = go(psum.at[2, half], r1m.at[half], s_near, second[half][1])
    forward("last")
    passed("last", last)
    n = width // CHUNK

    def span(j):
        return pl.ds(j * CHUNK, CHUNK)

    for j in range(n):
        sum_chip(last, j * CHUNK, (j + 1) * CHUNK)
        for half in range(2):
            flow["f", half, j] = go(
                psum.at[3, half, :, :, span(j)], r1f.at[half, :, :, span(j)], s_last, second[half][2]
            )

    x2 = []
    for kind in range(3):
        p, m = x1[kind]
        p.wait_recv()
        value = racc[kind, :, part_of(1)]
        xs2p[kind, hi] = value[hi].astype(BF16)
        xs2p[kind, lo] = (value[lo] + xr1p[kind].astype(F32)).astype(BF16)
        fp = go(xs2p.at[kind], xr2p.at[kind], s_x2p, xp)
        m.wait_recv()
        value = racc[kind, :, part_of(3)]
        xs2m[kind, lo] = value[lo].astype(BF16)
        xs2m[kind, hi] = (value[hi] + xr1m[kind].astype(F32)).astype(BF16)
        x2.append((fp, go(xs2m.at[kind], xr2m.at[kind], s_x2m, xm)))

    def add(*parts):
        total = parts[0].astype(F32)
        for part in parts[1:]:
            total += part.astype(F32)
        return total.astype(BF16)

    def second_sums(j):
        at = span(j)
        for half in range(2):
            if j == 0:
                flow["p", half].wait_recv()
                flow["m", half].wait_recv()
            flow["f", half, j].wait_recv()
            psum[0, half, :, :, at] = add(
                psum[0, half, :, :, at], r1p[half, :, :, at], r1m[half, :, :, at], r1f[half, :, :, at]
            )
            flow["r", half, j] = [
                go(psum.at[0, half, k1, :, at], dst.at[half, :, at], s_row, first[half][k])
                for k1, dst, k in ((3, r2f, 2), (1, r2p, 0), (2, r2m, 1))
            ]

    def first_sums(j):
        at = span(j)
        for half in range(2):
            for copy in flow["r", half, j]:
                copy.wait_recv()
            grad_out[half * 16 : half * 16 + 16, at] = add(
                psum[0, half, 0, :, at], r2p[half, :, at], r2m[half, :, at], r2f[half, :, at]
            )

    for j in range(n):
        second_sums(j)
        if j > 0:
            first_sums(j - 1)
    first_sums(n - 1)

    for kind in range(3):
        for copy in x2[kind]:
            copy.wait_recv()
        total = racc[kind, :, part_of(0)] + xr2p[kind].astype(F32) + xr2m[kind].astype(F32)
        rows_here[kind] = total.astype(BF16)
        bring(rows_here.at[kind], rows_out.at[kind])
    for copy in brought[-3:]:
        copy.wait()
    for s, total in groups:
        copy_of(total, total, s, recv.at[0], sib).wait_send()


def adam(live, rows, master, moment_one, moment_two, new_master, new_one, new_two):
    in_use = lax.broadcasted_iota(jnp.int32, rows.shape, 1) < live[0]
    row_grad = rows[...].astype(F32) * (1.0 / float(TOKENS) ** 0.5)
    m1, m2, weight = moment_one[...], moment_two[...], master[...]
    first = 0.9 * m1 + 0.1 * row_grad
    second = 0.95 * m2 + 0.05 * row_grad * row_grad
    step = first * (0.01 / (1.0 - 0.9**10)) / (jnp.sqrt(second * (1.0 / (1.0 - 0.95**10))) + 1e-08)
    new_master[...] = jnp.where(in_use, weight - step, weight)
    new_one[...] = jnp.where(in_use, first, m1)
    new_two[...] = jnp.where(in_use, second, m2)


def local(
    inputs, cotangent, w_gate, w_up, w_down, chosen, live_rows, master, moment_one, moment_two
):
    slots = chosen.shape[1]
    units, width = w_gate.shape
    grads = (4, 2, 4, 16, units)
    quarter = (3, slots, width // 4)
    half_quarter = (3, slots // 2, width // 4)
    any_space = pl.BlockSpec(memory_space=pl.ANY)
    vmem = pl.BlockSpec(memory_space=pltpu.VMEM)
    weight = pltpu.VMEM((units, width), BF16)
    state = tuple(jnp.transpose(a[0], (1, 0, 2)) for a in (master, moment_one, moment_two))
    wide = jax.ShapeDtypeStruct(quarter, F32)
    input_grad, row_grad = pl.pallas_call(
        kernel,
        out_shape=(jax.ShapeDtypeStruct((32, width), BF16), jax.ShapeDtypeStruct(quarter, BF16)),
        in_specs=[any_space] * 5 + [vmem],
        out_specs=(vmem, any_space),
        scratch_shapes=[
            pltpu.VMEM((2, 4, 2, 4, 2, 16, width), BF16),
            *[weight] * 5,
            *[pltpu.VMEM(grads, BF16)] * 6,
            pltpu.VMEM((3, slots, width), F32),
            *[pltpu.VMEM(quarter, BF16)] * 3,
            *[pltpu.VMEM(half_quarter, BF16)] * 2,
            *[pltpu.VMEM(quarter, BF16)] * 2,
            *[pltpu.VMEM((2, 4, 16, width), BF16)] * 3,
            *[pltpu.VMEM((2, 16, width), BF16)] * 3,
            pltpu.VMEM(quarter, BF16),
            pltpu.SemaphoreType.DMA((10,)),
            pltpu.SemaphoreType.DMA((SENDS,)),
            pltpu.SemaphoreType.DMA((RECEIVES,)),
        ],
        compiler_params=pltpu.CompilerParams(
            collective_id=0, has_side_effects=True, vmem_limit_bytes=58 * 1024 * 1024
        ),
    )(inputs, cotangent, w_gate, w_up, w_down, chosen)
    block = pl.BlockSpec((1, slots, ADAM_COLUMNS), lambda i, j: (i, 0, j))
    new = pl.pallas_call(
        adam,
        grid=(3, quarter[2] // ADAM_COLUMNS),
        compiler_params=pltpu.CompilerParams(vmem_limit_bytes=16 * 1024 * 1024),
        out_shape=(wide, wide, wide),
        in_specs=[pl.BlockSpec(memory_space=pltpu.SMEM)] + [block] * 4,
        out_specs=(block, block, block),
    )(live_rows, row_grad, *state)
    return (input_grad, *(jnp.transpose(a, (1, 0, 2))[None] for a in new))


def solution(mesh):
    token = P(("dp", "tensor", "opt"), None)
    hidden = P(("tensor", "opt"), None)
    state = P(("tensor", "opt"), None, None, "dp")
    return jax.shard_map(
        local,
        mesh=mesh,
        in_specs=(
            token, token, hidden, hidden, hidden, hidden, P(("tensor", "opt")), state, state, state,
        ),
        out_specs=(token, state, state, state),
        check_vma=False,
    )
```

```python
import jax
import jax.numpy as jnp
from jax import lax
from jax.experimental import pallas as pl
from jax.experimental.pallas import tpu as pltpu
from jax.sharding import PartitionSpec as P

MESH = pl.DeviceIdType.MESH
F32, BF16 = jnp.float32, jnp.bfloat16
NT = (((1,), (1,)), ((), ()))
CHUNK = 1024
TILE = 512
ORDER = (0, 1, 3, 2)
SENDS, RECEIVES = 16, 112
TOKENS = 4096
ADAM_COLUMNS = 1024


def kernel(
    inputs, cot, w_gate, w_up, w_down, chosen,
    grad_out, rows_out,
    xc, wg, wu, wd, wgs, wus, own_g, own_u, put_g, put_u, got_g, got_u,
    racc, xs1, xs2p, xs2m, xr1p, xr1m, xr2p, xr2m,
    r1p, r1m, r1f, r2p, r2m, r2f,
    rows_here, lsem, send, recv,
):
    dp, tz, op = lax.axis_index("dp"), lax.axis_index("tensor"), lax.axis_index("opt")
    y, core = op // 2, op % 2
    units, width = wg.shape
    slots = racc.shape[1]
    quarter = width // 4

    def on(i, k):
        return (i + k) % 4

    xp, xm = (on(dp, 1), tz, op), (on(dp, 3), tz, op)
    yp, ym, yf = ((dp, tz, on(y, k) * 2 + core) for k in (1, 3, 2))
    zp, zm, zf = ((dp, on(tz, k), op) for k in (1, 3, 2))
    sib = (dp, tz, y * 2 + 1 - core)
    first = ((yp, ym, yf), (zp, zm, zf))
    second = ((zp, zm, zf), (yp, ym, yf))

    psum = xc.at[0, :, :, :, 1]
    brought = []

    def bring(src, dst):
        copy = pltpu.make_async_copy(src, dst, lsem.at[len(brought)])
        copy.start()
        brought.append(copy)
        return copy

    mine = []
    for half in range(2):
        for kind, ref in enumerate((inputs, cot)):
            mine.append(bring(ref.at[pl.ds(half * 16, 16)], xc.at[kind, 0, half, 0, 0]))

    barrier = pltpu.get_barrier_semaphore()
    peers = (xp, xm, yp, ym, yf, zp, zm, zf, sib)
    for peer in peers:
        pl.semaphore_signal(barrier, inc=1, device_id=peer, device_id_type=MESH)
    pl.semaphore_wait(barrier, len(peers))

    groups, arrivals = [], []

    def group(total):
        groups.append((send.at[len(groups)], total))
        return groups[-1][0]

    def arrival():
        arrivals.append(None)
        return recv.at[len(arrivals) - 1]

    def copy_of(src, dst, s, r, device):
        return pltpu.make_async_remote_copy(
            src_ref=src, dst_ref=dst, send_sem=s, recv_sem=r, device_id=device, device_id_type=MESH
        )

    def go(src, dst, s, device, r=None):
        copy = copy_of(src, dst, s, arrival() if r is None else r, device)
        copy.start()
        return copy

    def all_of(dst, r):
        return copy_of(dst, dst, groups[0][0], r, sib)

    s_one = group(xc.at[0, 0, 0])
    s_two = group(xc.at[0, 0, 0, pl.ds(0, 2)])
    s_far = group(xc.at[:, 0])
    s_farther = group(xc.at[0, 0])
    s_share = group(xc.at[:, :, :, :, 0])
    s_wg, s_wu = group(wgs), group(wus)
    s_g, s_u = group(put_g), group(put_u)
    s_x1, s_x2p, s_x2m = group(xs1), group(xs2p), group(xs2m)
    s_near, s_last, s_row = group(psum.at[pl.ds(1, 2)]), group(psum.at[3]), group(psum.at[0, :, pl.ds(1, 3)])

    pieces = {
        "near": (slice(0, 1), slice(0, 4)),
        "mid0": (slice(1, 3), slice(0, 2)),
        "mid1": (slice(1, 3), slice(2, 4)),
        "last": (slice(3, 4), slice(0, 4)),
    }
    shared = {}
    for name in pieces:
        shared[name] = arrival()

    def ds(s):
        return pl.ds(s.start, s.stop - s.start)

    def piece_of(k2, k1):
        for name, (a, b) in pieces.items():
            if a.start <= k2 < a.stop and b.start <= k1 < b.stop:
                return name

    def slot(half, k2, k1):
        return xc.at[:, k2, half, k1, 0]

    def share(half, k2, k1):
        go(slot(half, k2, k1), xc.at[:, k2, half, k1, 1], s_share, sib, shared[piece_of(k2, k1)])

    one_p, one_m, two_in, two_cot = {}, {}, {}, {}
    far_p, far_m, far_in, far_cot = {}, {}, {}, {}

    def across(half, k1):
        here = slot(half, 0, k1)
        far_p[half, k1] = go(here, slot(half, 2, k1), s_far, second[half][0])
        far_m[half, k1] = go(here, slot(half, 1, k1), s_far, second[half][1])

    for half in range(2):
        for kind, ref in enumerate((inputs, cot)):
            here = ref.at[pl.ds(half * 16, 16)]
            one_p[half, kind] = go(here, xc.at[kind, 0, half, 2, 0], s_one, first[half][0])
            one_m[half, 1 - kind] = go(here, xc.at[kind, 0, half, 1, 0], s_one, first[half][1])
    for copy in mine:
        copy.wait()
    for half in range(2):
        across(half, 0)
    for half in range(2):
        share(half, 0, 0)
    sib_gate = go(w_gate, wgs, s_wg, sib)
    sib_up = go(w_up, wus, s_wu, sib)
    weights = [bring(w_gate, wg), bring(w_up, wu), bring(w_down, wd)]
    unit = lax.broadcasted_iota(jnp.int32, (512, slots), 0)
    pick = jnp.transpose((unit == chosen[...]).astype(F32))[:, :units].astype(BF16)
    for half in range(2):
        one_p[half, 0].wait_recv()
        two_in[half] = go(xc.at[0, 0, half, 2, 0], xc.at[0, 0, half, 3, 0], s_two, first[half][0])
        one_m[half, 0].wait_recv()
        two_cot[half] = go(xc.at[1, 0, half, 1, 0], xc.at[1, 0, half, 3, 0], s_two, first[half][1])
    for k1, side in ((1, one_m), (2, one_p)):
        for half in range(2):
            side[half, 1].wait_recv()
            across(half, k1)
            share(half, 0, k1)
    for half in range(2):
        two_in[half].wait_recv()
        two_cot[half].wait_recv()
        across(half, 3)
        share(half, 0, 3)

    sums = {"near": (arrival(), arrival()), "mid": (arrival(), arrival()), "last": (arrival(), arrival())}

    def part_of(k):
        return pl.ds(pl.multiple_of(on(dp, k) * quarter, quarter), quarter)

    lo, hi = slice(0, slots // 2), slice(slots // 2, slots)
    x1, x2 = {}, {}

    def x_first(kind):
        x1[kind] = (
            go(xs1.at[kind, ds(lo)], xr1p.at[kind], s_x1, xp),
            go(xs1.at[kind, ds(hi)], xr1m.at[kind], s_x1, xm),
        )

    def forward(name):
        a, b = pieces[name]
        na, nb = a.stop - a.start, b.stop - b.start
        tokens = na * 2 * nb * 2 * 16
        all_of(xc.at[:, ds(a), :, ds(b), 1], shared[name]).wait_recv()
        x = xc[0, a, :, b].reshape(tokens, width)
        c = xc[1, a, :, b].reshape(tokens, width)
        ends = sums[name.rstrip("01")]
        picked = [0.0, 0.0, 0.0]
        for u in (slice(0, 256), slice(256, units)):
            gate = lax.dot_general(x, wg[u], NT, preferred_element_type=F32)
            upv = lax.dot_general(x, wu[u], NT, preferred_element_type=F32)
            back = lax.dot_general(c, wd[u], NT, preferred_element_type=F32)
            sig = jax.nn.sigmoid(gate)
            activ = gate * sig
            hid = (activ * upv).astype(BF16)
            gg = (back * upv * sig * (1.0 + gate * (1.0 - sig))).astype(BF16)
            ug = (back * activ).astype(BF16)
            for value, own, put in ((gg, own_g, put_g), (ug, own_u, put_u)):
                split = value.reshape(na * 2 * nb, 2, 16, u.stop - u.start)
                own[a, :, b, :, u] = split[:, 0].reshape(na, 2, nb, 16, u.stop - u.start)
                put[a, :, b, :, u] = split[:, 1].reshape(na, 2, nb, 16, u.stop - u.start)
            for i, value in enumerate((gg, ug, hid)):
                picked[i] += lax.dot_general(pick[:, u], value, NT, preferred_element_type=F32)
        for put, got, s, r in ((put_g, got_g, s_g, ends[0]), (put_u, got_u, s_u, ends[1])):
            for k2 in range(a.start, a.stop):
                go(put.at[k2, :, ds(b)], got.at[k2, :, ds(b)], s, sib, r)
        picked = [value.astype(BF16) for value in picked]
        both = jnp.concatenate(picked[:2], axis=0)
        if name != "last":
            part = jnp.dot(both, x, preferred_element_type=F32).reshape(2, slots, width)
            down = jnp.dot(picked[2], c, preferred_element_type=F32)
            if name == "near":
                racc[0:2] = part
                racc[2] = down
            else:
                racc[0:2] += part
                racc[2] += down
            return
        for kinds, source, values in (((2,), 1, picked[2]), ((0, 1), 0, both)):
            for k in (2, 1, 3, 0):
                at = part_of(k)
                rows = xc[source, a, :, b, :, :, at].reshape(tokens, quarter)
                part = jnp.dot(values, rows, preferred_element_type=F32).reshape(len(kinds), slots, quarter)
                for i, kind in enumerate(kinds):
                    total = racc[kind, :, at] + part[i]
                    if k == 2:
                        xs1[kind] = total.astype(BF16)
                    else:
                        racc[kind, :, at] = total
                if k == 2:
                    x_first(kinds[0])
        x_first(1)

    def sum_chip(a, start, stop):
        rows = (a.stop - a.start) * 128
        size = TILE * 256 // rows

        def tile(i, carry):
            at = pl.ds(pl.multiple_of(start + i * size, size), size)
            total = 0.0
            for grads, weight in ((own_g, wg), (own_u, wu), (got_g, wgs), (got_u, wus)):
                total += jnp.dot(grads[a].reshape(rows, units), weight[:, at], preferred_element_type=F32)
            psum[a, :, :, :, at] = total.astype(BF16).reshape(a.stop - a.start, 2, 4, 16, size)
            return carry

        lax.fori_loop(0, (stop - start) // size, tile, 0)

    def passed(name, a):
        for got, r in zip((got_g, got_u), sums[name]):
            all_of(got.at[ds(a)], r).wait_recv()

    def onward(k1):
        for half in range(2):
            far_p[half, k1].wait_recv()
            far_in[half, k1] = go(xc.at[0, 2, half, k1, 0], xc.at[0, 3, half, k1, 0], s_farther, second[half][0])
            share(half, 2, k1)
            far_m[half, k1].wait_recv()
            far_cot[half, k1] = go(xc.at[1, 1, half, k1, 0], xc.at[1, 3, half, k1, 0], s_farther, second[half][1])
            share(half, 1, k1)

    def landed(k1):
        for half in range(2):
            far_in[half, k1].wait_recv()
            far_cot[half, k1].wait_recv()
            share(half, 3, k1)

    near, mid, last = slice(0, 1), slice(1, 3), slice(3, 4)
    for copy in weights:
        copy.wait()
    forward("near")
    onward(0)
    passed("near", near)
    sib_gate.wait_recv()
    sib_up.wait_recv()
    sum_chip(near, 0, width)
    onward(1)
    forward("mid0")
    onward(2)
    onward(3)
    forward("mid1")
    landed(0)
    landed(1)
    passed("mid", mid)
    flow = {}

    def send_near(start, stop):
        at = pl.ds(start, stop - start)
        for half in range(2):
            for side, (k2, dst) in enumerate(((1, r1p), (2, r1m))):
                flow[side, half, start] = go(
                    psum.at[k2, half, :, :, at], dst.at[half, :, :, at], s_near, second[half][side]
                )

    landed(2)
    landed(3)
    sum_chip(mid, 0, width // 2)
    send_near(0, width // 2)
    sum_chip(mid, width // 2, width)
    send_near(width // 2, width)
    forward("last")
    passed("last", last)
    n = width // CHUNK

    def span(j):
        return pl.ds(j * CHUNK, CHUNK)

    def sum_last(j):
        sum_chip(last, j * CHUNK, (j + 1) * CHUNK)

    def send_last(j):
        for half in range(2):
            flow["f", half, j] = go(
                psum.at[3, half, :, :, span(j)], r1f.at[half, :, :, span(j)], s_last, second[half][2]
            )

    def x_second(kind):
        p, m = x1[kind]
        p.wait_recv()
        value = racc[kind, :, part_of(1)]
        xs2p[kind, hi] = value[hi].astype(BF16)
        xs2p[kind, lo] = (value[lo] + xr1p[kind].astype(F32)).astype(BF16)
        fp = go(xs2p.at[kind], xr2p.at[kind], s_x2p, xp)
        m.wait_recv()
        value = racc[kind, :, part_of(3)]
        xs2m[kind, lo] = value[lo].astype(BF16)
        xs2m[kind, hi] = (value[hi] + xr1m[kind].astype(F32)).astype(BF16)
        x2[kind] = (fp, go(xs2m.at[kind], xr2m.at[kind], s_x2m, xm))

    def add(*parts):
        total = parts[0].astype(F32)
        for part in parts[1:]:
            total += part.astype(F32)
        return total.astype(BF16)

    def second_sums(j):
        at = span(j)
        for half in range(2):
            for side in range(2):
                if (side, half, j * CHUNK) in flow:
                    flow[side, half, j * CHUNK].wait_recv()
            flow["f", half, j].wait_recv()
            psum[0, half, :, :, at] = add(
                psum[0, half, :, :, at], r1p[half, :, :, at], r1m[half, :, :, at], r1f[half, :, :, at]
            )
            flow["r", half, j] = [
                go(psum.at[0, half, k1, :, at], dst.at[half, :, at], s_row, first[half][k])
                for k1, dst, k in ((3, r2f, 2), (1, r2p, 0), (2, r2m, 1))
            ]

    def first_sums(j):
        at = span(j)
        for half in range(2):
            for copy in flow["r", half, j]:
                copy.wait_recv()
            grad_out[half * 16 : half * 16 + 16, at] = add(
                psum[0, half, 0, :, at], r2p[half, :, at], r2m[half, :, at], r2f[half, :, at]
            )

    sum_last(0)
    send_last(0)
    x_second(2)
    sum_last(1)
    send_last(1)
    x_second(0)
    sum_last(2)
    x_second(1)
    for j in range(n):
        second_sums(j)
        if j + 2 < n:
            send_last(j + 2)
        if j + 3 < n:
            sum_last(j + 3)
        if j > 1:
            first_sums(j - 2)
    for j in range(n - 2, n):
        first_sums(j)
    for kind in (2, 0, 1):
        for copy in x2[kind]:
            copy.wait_recv()
        total = racc[kind, :, part_of(0)] + xr2p[kind].astype(F32) + xr2m[kind].astype(F32)
        rows_here[kind] = total.astype(BF16)
        bring(rows_here.at[kind], rows_out.at[kind])
    for copy in brought[-3:]:
        copy.wait()
    for s, total in groups:
        copy_of(total, total, s, recv.at[0], sib).wait_send()


def adam(live, rows, master, moment_one, moment_two, new_master, new_one, new_two):
    in_use = lax.broadcasted_iota(jnp.int32, rows.shape, 1) < live[0]
    row_grad = rows[...].astype(F32) * (1.0 / float(TOKENS) ** 0.5)
    m1, m2, weight = moment_one[...], moment_two[...], master[...]
    first = 0.9 * m1 + 0.1 * row_grad
    second = 0.95 * m2 + 0.05 * row_grad * row_grad
    step = first * (0.01 / (1.0 - 0.9**10)) / (jnp.sqrt(second * (1.0 / (1.0 - 0.95**10))) + 1e-08)
    new_master[...] = jnp.where(in_use, weight - step, weight)
    new_one[...] = jnp.where(in_use, first, m1)
    new_two[...] = jnp.where(in_use, second, m2)


def local(
    inputs, cotangent, w_gate, w_up, w_down, chosen, live_rows, master, moment_one, moment_two
):
    slots = chosen.shape[1]
    units, width = w_gate.shape
    grads = (4, 2, 4, 16, units)
    quarter = (3, slots, width // 4)
    half_quarter = (3, slots // 2, width // 4)
    any_space = pl.BlockSpec(memory_space=pl.ANY)
    vmem = pl.BlockSpec(memory_space=pltpu.VMEM)
    weight = pltpu.VMEM((units, width), BF16)
    state = tuple(jnp.transpose(a[0], (1, 0, 2)) for a in (master, moment_one, moment_two))
    wide = jax.ShapeDtypeStruct(quarter, F32)
    input_grad, row_grad = pl.pallas_call(
        kernel,
        out_shape=(jax.ShapeDtypeStruct((32, width), BF16), jax.ShapeDtypeStruct(quarter, BF16)),
        in_specs=[any_space] * 5 + [vmem],
        out_specs=(vmem, any_space),
        scratch_shapes=[
            pltpu.VMEM((2, 4, 2, 4, 2, 16, width), BF16),
            *[weight] * 5,
            *[pltpu.VMEM(grads, BF16)] * 6,
            pltpu.VMEM((3, slots, width), F32),
            *[pltpu.VMEM(quarter, BF16)] * 3,
            *[pltpu.VMEM(half_quarter, BF16)] * 2,
            *[pltpu.VMEM(quarter, BF16)] * 2,
            *[pltpu.VMEM((2, 4, 16, width), BF16)] * 3,
            *[pltpu.VMEM((2, 16, width), BF16)] * 3,
            pltpu.VMEM(quarter, BF16),
            pltpu.SemaphoreType.DMA((10,)),
            pltpu.SemaphoreType.DMA((SENDS,)),
            pltpu.SemaphoreType.DMA((RECEIVES,)),
        ],
        compiler_params=pltpu.CompilerParams(
            collective_id=0, has_side_effects=True, vmem_limit_bytes=58 * 1024 * 1024
        ),
    )(inputs, cotangent, w_gate, w_up, w_down, chosen)
    block = pl.BlockSpec((1, slots, ADAM_COLUMNS), lambda i, j: (i, 0, j))
    new = pl.pallas_call(
        adam,
        grid=(3, quarter[2] // ADAM_COLUMNS),
        compiler_params=pltpu.CompilerParams(vmem_limit_bytes=16 * 1024 * 1024),
        out_shape=(wide, wide, wide),
        in_specs=[pl.BlockSpec(memory_space=pltpu.SMEM)] + [block] * 4,
        out_specs=(block, block, block),
    )(live_rows, row_grad, *state)
    return (input_grad, *(jnp.transpose(a, (1, 0, 2))[None] for a in new))


def solution(mesh):
    token = P(("dp", "tensor", "opt"), None)
    hidden = P(("tensor", "opt"), None)
    state = P(("tensor", "opt"), None, None, "dp")
    return jax.shard_map(
        local,
        mesh=mesh,
        in_specs=(
            token, token, hidden, hidden, hidden, hidden, P(("tensor", "opt")), state, state, state,
        ),
        out_specs=(token, state, state, state),
        check_vma=False,
    )
```

```python
import jax
import jax.numpy as jnp
from jax import lax
from jax.experimental import pallas as pl
from jax.experimental.pallas import tpu as pltpu
from jax.sharding import PartitionSpec as P

MESH = pl.DeviceIdType.MESH
F32, BF16 = jnp.float32, jnp.bfloat16
NT = (((1,), (1,)), ((), ()))
CHUNK = 1024
TILE = 512
ORDER = (0, 1, 3, 2)
SENDS, RECEIVES = 16, 112
TOKENS = 4096
ADAM_COLUMNS = 1024


def kernel(
    inputs, cot, w_gate, w_up, w_down, chosen,
    grad_out, rows_out,
    xc, wg, wu, wd, wgs, wus, own_g, own_u, put_g, put_u, got_g, got_u,
    racc, xs1, xs2p, xs2m, xr1p, xr1m, xr2p, xr2m,
    r1p, r1m, r1f, r2p, r2m, r2f,
    rows_here, lsem, send, recv,
):
    dp, tz, op = lax.axis_index("dp"), lax.axis_index("tensor"), lax.axis_index("opt")
    y, core = op // 2, op % 2
    units, width = wg.shape
    slots = racc.shape[1]
    quarter = width // 4

    def on(i, k):
        return (i + k) % 4

    xp, xm = (on(dp, 1), tz, op), (on(dp, 3), tz, op)
    yp, ym, yf = ((dp, tz, on(y, k) * 2 + core) for k in (1, 3, 2))
    zp, zm, zf = ((dp, on(tz, k), op) for k in (1, 3, 2))
    sib = (dp, tz, y * 2 + 1 - core)
    first = ((yp, ym, yf), (zp, zm, zf))
    second = ((zp, zm, zf), (yp, ym, yf))

    psum = xc.at[0, :, :, :, 1]
    brought = []

    def bring(src, dst):
        copy = pltpu.make_async_copy(src, dst, lsem.at[len(brought)])
        copy.start()
        brought.append(copy)
        return copy

    mine = []
    for half in range(2):
        for kind, ref in enumerate((inputs, cot)):
            mine.append(bring(ref.at[pl.ds(half * 16, 16)], xc.at[kind, 0, half, 0, 0]))

    barrier = pltpu.get_barrier_semaphore()
    peers = (xp, xm, yp, ym, yf, zp, zm, zf, sib)
    for peer in peers:
        pl.semaphore_signal(barrier, inc=1, device_id=peer, device_id_type=MESH)
    pl.semaphore_wait(barrier, len(peers))

    groups, arrivals = [], []

    def group(total):
        groups.append((send.at[len(groups)], total))
        return groups[-1][0]

    def arrival():
        arrivals.append(None)
        return recv.at[len(arrivals) - 1]

    def copy_of(src, dst, s, r, device):
        return pltpu.make_async_remote_copy(
            src_ref=src, dst_ref=dst, send_sem=s, recv_sem=r, device_id=device, device_id_type=MESH
        )

    def go(src, dst, s, device, r=None):
        copy = copy_of(src, dst, s, arrival() if r is None else r, device)
        copy.start()
        return copy

    def all_of(dst, r):
        return copy_of(dst, dst, groups[0][0], r, sib)

    s_one = group(xc.at[0, 0, 0])
    s_two = group(xc.at[0, 0, 0, pl.ds(0, 2)])
    s_far = group(xc.at[:, 0])
    s_farther = group(xc.at[0, 0])
    s_share = group(xc.at[:, :, :, :, 0])
    s_wg, s_wu = group(wgs), group(wus)
    s_g, s_u = group(put_g), group(put_u)
    s_x1, s_x2p, s_x2m = group(xs1), group(xs2p), group(xs2m)
    s_near, s_last, s_row = group(psum.at[pl.ds(1, 2)]), group(psum.at[3]), group(psum.at[0, :, pl.ds(1, 3)])

    pieces = {
        "near": (slice(0, 1), slice(0, 4)),
        "mid0": (slice(1, 3), slice(0, 2)),
        "mid1": (slice(1, 3), slice(2, 4)),
        "last": (slice(3, 4), slice(0, 4)),
    }
    shared = {}
    for name in pieces:
        shared[name] = arrival()

    def ds(s):
        return pl.ds(s.start, s.stop - s.start)

    def piece_of(k2, k1):
        for name, (a, b) in pieces.items():
            if a.start <= k2 < a.stop and b.start <= k1 < b.stop:
                return name

    def slot(half, k2, k1):
        return xc.at[:, k2, half, k1, 0]

    def share(half, k2, k1):
        go(slot(half, k2, k1), xc.at[:, k2, half, k1, 1], s_share, sib, shared[piece_of(k2, k1)])

    one_p, one_m, two_in, two_cot = {}, {}, {}, {}
    far_p, far_m, far_in, far_cot = {}, {}, {}, {}

    def across(half, k1):
        here = slot(half, 0, k1)
        far_p[half, k1] = go(here, slot(half, 2, k1), s_far, second[half][0])
        far_m[half, k1] = go(here, slot(half, 1, k1), s_far, second[half][1])

    for half in range(2):
        for kind, ref in enumerate((inputs, cot)):
            here = ref.at[pl.ds(half * 16, 16)]
            one_p[half, kind] = go(here, xc.at[kind, 0, half, 2, 0], s_one, first[half][0])
            one_m[half, 1 - kind] = go(here, xc.at[kind, 0, half, 1, 0], s_one, first[half][1])
    for copy in mine:
        copy.wait()
    for half in range(2):
        across(half, 0)
    for half in range(2):
        share(half, 0, 0)
    sib_gate = go(w_gate, wgs, s_wg, sib)
    sib_up = go(w_up, wus, s_wu, sib)
    weights = [bring(w_gate, wg), bring(w_up, wu), bring(w_down, wd)]
    unit = lax.broadcasted_iota(jnp.int32, (512, slots), 0)
    pick = jnp.transpose((unit == chosen[...]).astype(F32))[:, :units].astype(BF16)
    for half in range(2):
        one_p[half, 0].wait_recv()
        two_in[half] = go(xc.at[0, 0, half, 2, 0], xc.at[0, 0, half, 3, 0], s_two, first[half][0])
        one_m[half, 0].wait_recv()
        two_cot[half] = go(xc.at[1, 0, half, 1, 0], xc.at[1, 0, half, 3, 0], s_two, first[half][1])
    for k1, side in ((1, one_m), (2, one_p)):
        for half in range(2):
            side[half, 1].wait_recv()
            across(half, k1)
            share(half, 0, k1)
    for half in range(2):
        two_in[half].wait_recv()
        two_cot[half].wait_recv()
        across(half, 3)
        share(half, 0, 3)

    sums = {"near": (arrival(), arrival()), "mid": (arrival(), arrival()), "last": (arrival(), arrival())}

    def part_of(k):
        return pl.ds(pl.multiple_of(on(dp, k) * quarter, quarter), quarter)

    lo, hi = slice(0, slots // 2), slice(slots // 2, slots)
    x1, x2 = {}, {}

    def x_first(kind):
        x1[kind] = (
            go(xs1.at[kind, ds(lo)], xr1p.at[kind], s_x1, xp),
            go(xs1.at[kind, ds(hi)], xr1m.at[kind], s_x1, xm),
        )

    def forward(name):
        a, b = pieces[name]
        na, nb = a.stop - a.start, b.stop - b.start
        tokens = na * 2 * nb * 2 * 16
        all_of(xc.at[:, ds(a), :, ds(b), 1], shared[name]).wait_recv()
        x = xc[0, a, :, b].reshape(tokens, width)
        c = xc[1, a, :, b].reshape(tokens, width)
        ends = sums[name.rstrip("01")]
        picked = [0.0, 0.0, 0.0]
        for u in (slice(0, 256), slice(256, units)):
            gate = lax.dot_general(x, wg[u], NT, preferred_element_type=F32)
            upv = lax.dot_general(x, wu[u], NT, preferred_element_type=F32)
            back = lax.dot_general(c, wd[u], NT, preferred_element_type=F32)
            sig = jax.nn.sigmoid(gate)
            activ = gate * sig
            hid = (activ * upv).astype(BF16)
            gg = (back * upv * sig * (1.0 + gate * (1.0 - sig))).astype(BF16)
            ug = (back * activ).astype(BF16)
            for value, own, put in ((gg, own_g, put_g), (ug, own_u, put_u)):
                split = value.reshape(na * 2 * nb, 2, 16, u.stop - u.start)
                own[a, :, b, :, u] = split[:, 0].reshape(na, 2, nb, 16, u.stop - u.start)
                put[a, :, b, :, u] = split[:, 1].reshape(na, 2, nb, 16, u.stop - u.start)
            for i, value in enumerate((gg, ug, hid)):
                picked[i] += lax.dot_general(pick[:, u], value, NT, preferred_element_type=F32)
        for put, got, s, r in ((put_g, got_g, s_g, ends[0]), (put_u, got_u, s_u, ends[1])):
            for k2 in range(a.start, a.stop):
                go(put.at[k2, :, ds(b)], got.at[k2, :, ds(b)], s, sib, r)
        picked = [value.astype(BF16) for value in picked]
        both = jnp.concatenate(picked[:2], axis=0)
        if name != "last":
            part = jnp.dot(both, x, preferred_element_type=F32).reshape(2, slots, width)
            down = jnp.dot(picked[2], c, preferred_element_type=F32)
            if name == "near":
                racc[0:2] = part
                racc[2] = down
            else:
                racc[0:2] += part
                racc[2] += down
            return
        for kinds, source, values in (((2,), 1, picked[2]), ((0, 1), 0, both)):
            for k in (2, 1, 3, 0):
                at = part_of(k)
                rows = xc[source, a, :, b, :, :, at].reshape(tokens, quarter)
                part = jnp.dot(values, rows, preferred_element_type=F32).reshape(len(kinds), slots, quarter)
                for i, kind in enumerate(kinds):
                    total = racc[kind, :, at] + part[i]
                    if k == 2:
                        xs1[kind] = total.astype(BF16)
                    else:
                        racc[kind, :, at] = total
                if k == 2:
                    x_first(kinds[0])
        x_first(1)

    def sum_chip(a, start, stop):
        rows = (a.stop - a.start) * 128
        size = TILE * 256 // rows

        def tile(i, carry):
            at = pl.ds(pl.multiple_of(start + i * size, size), size)
            total = 0.0
            for grads, weight in ((own_g, wg), (own_u, wu), (got_g, wgs), (got_u, wus)):
                total += jnp.dot(grads[a].reshape(rows, units), weight[:, at], preferred_element_type=F32)
            psum[a, :, :, :, at] = total.astype(BF16).reshape(a.stop - a.start, 2, 4, 16, size)
            return carry

        lax.fori_loop(0, (stop - start) // size, tile, 0)

    def passed(name, a):
        for got, r in zip((got_g, got_u), sums[name]):
            all_of(got.at[ds(a)], r).wait_recv()

    def onward(k1):
        for half in range(2):
            far_p[half, k1].wait_recv()
            far_in[half, k1] = go(xc.at[0, 2, half, k1, 0], xc.at[0, 3, half, k1, 0], s_farther, second[half][0])
            share(half, 2, k1)
            far_m[half, k1].wait_recv()
            far_cot[half, k1] = go(xc.at[1, 1, half, k1, 0], xc.at[1, 3, half, k1, 0], s_farther, second[half][1])
            share(half, 1, k1)

    def landed(k1):
        for half in range(2):
            far_in[half, k1].wait_recv()
            far_cot[half, k1].wait_recv()
            share(half, 3, k1)

    near, mid, last = slice(0, 1), slice(1, 3), slice(3, 4)
    for copy in weights:
        copy.wait()
    forward("near")
    onward(0)
    passed("near", near)
    sib_gate.wait_recv()
    sib_up.wait_recv()
    sum_chip(near, 0, width)
    onward(1)
    forward("mid0")
    onward(2)
    onward(3)
    forward("mid1")
    landed(0)
    landed(1)
    passed("mid", mid)
    flow = {}

    def send_near(start, stop):
        at = pl.ds(start, stop - start)
        for half in range(2):
            for side, (k2, dst) in enumerate(((1, r1p), (2, r1m))):
                flow[side, half, start] = go(
                    psum.at[k2, half, :, :, at], dst.at[half, :, :, at], s_near, second[half][side]
                )

    landed(2)
    landed(3)
    sum_chip(mid, 0, width // 2)
    send_near(0, width // 2)
    sum_chip(mid, width // 2, width)
    send_near(width // 2, width)
    forward("last")
    passed("last", last)
    n = width // CHUNK

    def span(j):
        return pl.ds(j * CHUNK, CHUNK)

    def sum_last(j):
        sum_chip(last, j * CHUNK, (j + 1) * CHUNK)

    def send_last(j):
        for half in range(2):
            flow["f", half, j] = go(
                psum.at[3, half, :, :, span(j)], r1f.at[half, :, :, span(j)], s_last, second[half][2]
            )

    def x_second(kind):
        p, m = x1[kind]
        p.wait_recv()
        value = racc[kind, :, part_of(1)]
        xs2p[kind, hi] = value[hi].astype(BF16)
        xs2p[kind, lo] = (value[lo] + xr1p[kind].astype(F32)).astype(BF16)
        fp = go(xs2p.at[kind], xr2p.at[kind], s_x2p, xp)
        m.wait_recv()
        value = racc[kind, :, part_of(3)]
        xs2m[kind, lo] = value[lo].astype(BF16)
        xs2m[kind, hi] = (value[hi] + xr1m[kind].astype(F32)).astype(BF16)
        x2[kind] = (fp, go(xs2m.at[kind], xr2m.at[kind], s_x2m, xm))

    def add(*parts):
        total = parts[0].astype(F32)
        for part in parts[1:]:
            total += part.astype(F32)
        return total.astype(BF16)

    def second_sums(j):
        at = span(j)
        for half in range(2):
            for side in range(2):
                if (side, half, j * CHUNK) in flow:
                    flow[side, half, j * CHUNK].wait_recv()
            flow["f", half, j].wait_recv()
            psum[0, half, :, :, at] = add(
                psum[0, half, :, :, at], r1p[half, :, :, at], r1m[half, :, :, at], r1f[half, :, :, at]
            )
            flow["r", half, j] = [
                go(psum.at[0, half, k1, :, at], dst.at[half, :, at], s_row, first[half][k])
                for k1, dst, k in ((3, r2f, 2), (1, r2p, 0), (2, r2m, 1))
            ]

    def first_sums(j):
        at = span(j)
        for half in range(2):
            for copy in flow["r", half, j]:
                copy.wait_recv()
            grad_out[half * 16 : half * 16 + 16, at] = add(
                psum[0, half, 0, :, at], r2p[half, :, at], r2m[half, :, at], r2f[half, :, at]
            )

    sum_last(0)
    send_last(0)
    x_second(2)
    sum_last(1)
    send_last(1)
    x_second(0)
    sum_last(2)
    x_second(1)
    for j in range(n):
        second_sums(j)
        if j + 2 < n:
            send_last(j + 2)
        if j + 3 < n:
            sum_last(j + 3)
        if j > 1:
            first_sums(j - 2)
    for j in range(n - 2, n):
        first_sums(j)
    for kind in (2, 0, 1):
        for copy in x2[kind]:
            copy.wait_recv()
        total = racc[kind, :, part_of(0)] + xr2p[kind].astype(F32) + xr2m[kind].astype(F32)
        rows_here[kind] = total.astype(BF16)
        bring(rows_here.at[kind], rows_out.at[kind])
    for copy in brought[-3:]:
        copy.wait()
    for s, total in groups:
        copy_of(total, total, s, recv.at[0], sib).wait_send()


def adam(live, all_rows, master, moment_one, moment_two, new_master, new_one, new_two, rows, sems):
    kind = pl.program_id(0)

    @pl.when(kind == 0)
    def _():
        for i in range(3):
            pltpu.make_async_copy(all_rows.at[i], rows.at[i], sems.at[i]).start()

    pltpu.make_async_copy(all_rows.at[kind], rows.at[kind], sems.at[kind]).wait()
    in_use = lax.broadcasted_iota(jnp.int32, master.shape, 1) < live[0]
    row_grad = rows[pl.ds(kind, 1)].astype(F32) * (1.0 / float(TOKENS) ** 0.5)
    m1, m2, weight = moment_one[...], moment_two[...], master[...]
    first = 0.9 * m1 + 0.1 * row_grad
    second = 0.95 * m2 + 0.05 * row_grad * row_grad
    step = first * (0.01 / (1.0 - 0.9**10)) / (jnp.sqrt(second * (1.0 / (1.0 - 0.95**10))) + 1e-08)
    new_master[...] = jnp.where(in_use, weight - step, weight)
    new_one[...] = jnp.where(in_use, first, m1)
    new_two[...] = jnp.where(in_use, second, m2)


def local(
    inputs, cotangent, w_gate, w_up, w_down, chosen, live_rows, master, moment_one, moment_two
):
    slots = chosen.shape[1]
    units, width = w_gate.shape
    grads = (4, 2, 4, 16, units)
    quarter = (3, slots, width // 4)
    half_quarter = (3, slots // 2, width // 4)
    any_space = pl.BlockSpec(memory_space=pl.ANY)
    vmem = pl.BlockSpec(memory_space=pltpu.VMEM)
    weight = pltpu.VMEM((units, width), BF16)
    state = tuple(jnp.transpose(a[0], (1, 0, 2)) for a in (master, moment_one, moment_two))
    wide = jax.ShapeDtypeStruct(quarter, F32)
    input_grad, row_grad = pl.pallas_call(
        kernel,
        out_shape=(jax.ShapeDtypeStruct((32, width), BF16), jax.ShapeDtypeStruct(quarter, BF16)),
        in_specs=[any_space] * 5 + [vmem],
        out_specs=(vmem, any_space),
        scratch_shapes=[
            pltpu.VMEM((2, 4, 2, 4, 2, 16, width), BF16),
            *[weight] * 5,
            *[pltpu.VMEM(grads, BF16)] * 6,
            pltpu.VMEM((3, slots, width), F32),
            *[pltpu.VMEM(quarter, BF16)] * 3,
            *[pltpu.VMEM(half_quarter, BF16)] * 2,
            *[pltpu.VMEM(quarter, BF16)] * 2,
            *[pltpu.VMEM((2, 4, 16, width), BF16)] * 3,
            *[pltpu.VMEM((2, 16, width), BF16)] * 3,
            pltpu.VMEM(quarter, BF16),
            pltpu.SemaphoreType.DMA((10,)),
            pltpu.SemaphoreType.DMA((SENDS,)),
            pltpu.SemaphoreType.DMA((RECEIVES,)),
        ],
        compiler_params=pltpu.CompilerParams(
            collective_id=0, has_side_effects=True, vmem_limit_bytes=58 * 1024 * 1024
        ),
    )(inputs, cotangent, w_gate, w_up, w_down, chosen)
    block = pl.BlockSpec((1, slots, ADAM_COLUMNS), lambda i, j: (i, 0, j))
    new = pl.pallas_call(
        adam,
        grid=(3, quarter[2] // ADAM_COLUMNS),
        compiler_params=pltpu.CompilerParams(vmem_limit_bytes=16 * 1024 * 1024),
        out_shape=(wide, wide, wide),
        in_specs=[pl.BlockSpec(memory_space=pltpu.SMEM), pl.BlockSpec(memory_space=pltpu.HBM)] + [block] * 3,
        out_specs=(block, block, block),
        scratch_shapes=[pltpu.VMEM(quarter, BF16), pltpu.SemaphoreType.DMA((3,))],
    )(live_rows, row_grad, *state)
    return (input_grad, *(jnp.transpose(a, (1, 0, 2))[None] for a in new))


def solution(mesh):
    token = P(("dp", "tensor", "opt"), None)
    hidden = P(("tensor", "opt"), None)
    state = P(("tensor", "opt"), None, None, "dp")
    return jax.shard_map(
        local,
        mesh=mesh,
        in_specs=(
            token, token, hidden, hidden, hidden, hidden, P(("tensor", "opt")), state, state, state,
        ),
        out_specs=(token, state, state, state),
        check_vma=False,
    )
```
